32 devices in a mesh: groups: 2 (over y), blk: 4 (over z), heads: 2 (over x), section: 2 (over core).
Axes of the slice: x: 2, y: 2, z: 4, core: 2. Of those that a mesh axis runs over, the one named last changes fastest.
Arguments:
- dec_states: bfloat16 [4096, 2304], P(('groups', 'blk', 'section')), parts along dimension 0, may hold values from -6 to 6
- cross_keys: bfloat16 [1024, 1, 256], P(('groups', 'blk')), parts along dimension 0, may hold values from -15 to 15
- cross_values: bfloat16 [1024, 1, 256], P(('groups', 'blk')), parts along dimension 0, may hold values from -6 to 6
- attn_gain: float32 [2304], replicated, may hold values from 0.1 to 1.9
- query_weight: bfloat16 [2304, 512], P(None, 'heads'), may hold values from -0.125 to 0.125
- out_weight: bfloat16 [512, 2304], P('heads'), may hold values from -0.25 to 0.25
- post_attn_gain: float32 [2304], replicated, may hold values from 0.1 to 1.9
- ffn_gain: float32 [2304], replicated, may hold values from 0.1 to 1.9
- gate_weight: bfloat16 [2304, 9216], P('blk', ('heads', 'section')), may hold values from -0.125 to 0.125
- up_weight: bfloat16 [2304, 9216], P('blk', ('heads', 'section')), may hold values from -0.125 to 0.125
- down_weight: bfloat16 [9216, 2304], P(('heads', 'section'), 'blk'), may hold values from -0.0625 to 0.0625
- post_ffn_gain: float32 [2304], replicated, may hold values from 0.1 to 1.9
Outputs:
- scored_states: bfloat16 [4096, 2304], P(('groups', 'blk', 'heads', 'section')), parts along dimension 0
The draws below stay inside these ranges and needn't reach their ends.
There are 2 independent parts, one for each index of `groups`. The reference program is written for one: setup_inputs(seed, part) draws one part's arguments, and reference() takes and returns one part's arrays. A program takes and returns all parts, laid end to end along the dimension named above; an argument that names none is the same for every part. Nothing has to cross between parts.
All inputs are finite; a program needn't handle non-finite values.
Results may differ from the reference program's by a relative error of at most 0.02.
Values may be sent and summed in bfloat16 or wider, within the bound.
No kernel may reach another device: no remote copies, remote signals or barrier semaphores. Data moves between devices by JAX's collectives and lax.ppermute only.
A program may use at most 128 MiB of HBM per device.

```python
import jax
import jax.numpy as jnp
from jax import lax

D = 2304
FF = 9216
HD = 256
GROUP = 2
HEADS = 2
KVH = 1
TGT = 2048
SRC = 512
N_HEADS = 2
N_SECTION = 2


def level_of(rng, extent, pieces, least, largest):
    factor_of, own = 1.0, jax.random.fold_in(rng, 6)
    for axis_at, shards_of in pieces:
        steps = jnp.exp(jax.random.uniform(jax.random.fold_in(own, axis_at), (shards_of,), jnp.float32, least / len(pieces), largest / len(pieces)))
        factor_of = factor_of * jnp.repeat(steps, extent[axis_at] // shards_of).reshape([-1 if axis == axis_at else 1 for axis in range(len(extent))])
    return factor_of


def centred(own_key, dims, deviation, reach, pieces=(), kind=jnp.bfloat16):
    entries = jax.random.normal(own_key, dims, jnp.float32) * deviation
    if len(pieces) > 0:
        entries = level_of(own_key, dims, pieces, -0.22, 0.18) * entries
    return jnp.clip(entries, min=-reach, max=reach).astype(kind)


def setup_inputs(seed: int = 0, part: int = 0) -> dict:
    splits = jax.random.split(jax.random.key(seed), 13)
    part_splits = jax.random.split(jax.random.fold_in(splits[12], part), 13)
    return {
        "dec_states": centred(part_splits[0], (TGT, D), 1.0, 6.0, ((0, 8),)),
        "cross_keys": centred(part_splits[1], (SRC, KVH, HD), 2.5, 15.0, ((0, 4),)),
        "cross_values": centred(part_splits[2], (SRC, KVH, HD), 1.0, 6.0, ((0, 4),)),
        "attn_gain": jnp.clip(1.0 + 0.18 * jax.random.normal(splits[3], (D,), jnp.float32), 0.1, 1.9),
        "query_weight": centred(splits[4], (D, HEADS * HD), D ** -0.5, 0.125, ((1, 2),)),
        "out_weight": centred(splits[5], (HEADS * HD, D), (HEADS * HD) ** -0.5, 0.25, ((0, 2),)),
        "post_attn_gain": jnp.clip(1.0 + 0.18 * jax.random.normal(splits[6], (D,), jnp.float32), 0.1, 1.9),
        "ffn_gain": jnp.clip(1.0 + 0.18 * jax.random.normal(splits[7], (D,), jnp.float32), 0.1, 1.9),
        "gate_weight": centred(splits[8], (D, FF), D ** -0.5, 0.125, ((0, 4), (1, 4))),
        "up_weight": centred(splits[9], (D, FF), D ** -0.5, 0.125, ((0, 4), (1, 4))),
        "down_weight": centred(splits[10], (FF, D), FF ** -0.5, 0.0625, ((0, 4), (1, 4))),
        "post_ffn_gain": jnp.clip(1.0 + 0.18 * jax.random.normal(splits[11], (D,), jnp.float32), 0.1, 1.9),
    }


softcap_limit = 50.0

def rms_scale(values, gain):
    return values * lax.rsqrt(lax.optimization_barrier(jnp.mean(values * values, axis=-1, keepdims=True)) + 1e-06) * gain

def reference(dec_states, cross_keys, cross_values, attn_gain, query_weight, out_weight, post_attn_gain, ffn_gain, gate_weight, up_weight, down_weight, post_ffn_gain):
    states = dec_states.astype(jnp.float32)
    normed = rms_scale(states, attn_gain).astype(jnp.bfloat16)
    queries = jnp.dot(normed, query_weight, preferred_element_type=jnp.float32).astype(jnp.bfloat16)

    def head_step(total, head):
        head_queries = lax.dynamic_slice_in_dim(queries, head * HD, HD, 1)
        kv_index = head // GROUP
        keys = lax.dynamic_index_in_dim(cross_keys, kv_index, 1, keepdims=False)
        values = lax.dynamic_index_in_dim(cross_values, kv_index, 1, keepdims=False)
        raw = lax.dot_general(head_queries, keys, (((1,), (1,)), ((), ())), preferred_element_type=jnp.float32) * HD ** (-0.5)
        scores = softcap_limit * jnp.tanh(raw / softcap_limit)
        probs = jnp.exp(scores)
        totals = lax.optimization_barrier(jnp.sum(probs, axis=1, keepdims=True))
        context = (jnp.dot(probs.astype(jnp.bfloat16), values, preferred_element_type=jnp.float32) / totals).astype(jnp.bfloat16)
        out_rows = lax.dynamic_slice_in_dim(out_weight, head * HD, HD, 0)
        term = jnp.dot(context, out_rows, preferred_element_type=jnp.float32).astype(jnp.bfloat16)
        term = lax.optimization_barrier(term)
        return (total + term.astype(jnp.float32), None)
    attended, unused = lax.scan(head_step, jnp.zeros((TGT, D), jnp.float32), jnp.arange(HEADS, dtype=jnp.int32))
    residual = (states + rms_scale(attended, post_attn_gain)).astype(jnp.bfloat16)
    ffn_input = rms_scale(residual.astype(jnp.float32), ffn_gain).astype(jnp.bfloat16)
    group_count = N_HEADS * N_SECTION
    group_units = FF // group_count

    def group_step(total, group):
        start = group * group_units
        gate = jnp.dot(ffn_input, lax.dynamic_slice_in_dim(gate_weight, start, group_units, 1), preferred_element_type=jnp.float32)
        up_part = jnp.dot(ffn_input, lax.dynamic_slice_in_dim(up_weight, start, group_units, 1), preferred_element_type=jnp.float32)
        hidden = (jax.nn.gelu(gate, approximate=True) * up_part).astype(jnp.bfloat16)
        term = jnp.dot(hidden, lax.dynamic_slice_in_dim(down_weight, start, group_units, 0), preferred_element_type=jnp.float32).astype(jnp.bfloat16)
        term = lax.optimization_barrier(term)
        return (total + term.astype(jnp.float32), None)
    ffn_out, unused_two = lax.scan(group_step, jnp.zeros((TGT, D), jnp.float32), jnp.arange(group_count, dtype=jnp.int32))
    return (residual.astype(jnp.float32) + rms_scale(ffn_out, post_ffn_gain)).astype(jnp.bfloat16)
```

```python
import jax
import jax.numpy as jnp
from jax import lax
from jax.sharding import PartitionSpec as P

HD = 256
GROUP = 2
LANE = 128


softcap_limit = 50.0


def from_partner(block, axis, bit):
    count = lax.axis_size(axis)
    route = []
    for low in range(count):
        high = low | 1 << bit
        if high != low and high < count:
            route += [(low, high), (high, low)]
    return lax.ppermute(block, axis, route)


def rms_scale(values, gain):
    return values * lax.rsqrt(jnp.mean(values * values, axis=-1, keepdims=True) + 1e-06) * gain


def capped_scores(queries, keys):
    raw = lax.dot_general(
        queries, keys, (((1,), (1,)), ((), ())), preferred_element_type=jnp.float32
    ) * HD ** (-0.5)
    return softcap_limit * jnp.tanh(raw / softcap_limit)


def gathered_body(
    dec_states,
    cross_keys,
    cross_values,
    attn_gain,
    query_weight,
    out_weight,
    post_attn_gain,
    ffn_gain,
    gate_weight,
    up_weight,
    down_weight,
    post_ffn_gain,
):
    head_index = lax.axis_index("heads")
    kv_index = head_index // GROUP
    keys_local = lax.dynamic_index_in_dim(cross_keys, kv_index, 1, keepdims=False)
    values_local = lax.dynamic_index_in_dim(cross_values, kv_index, 1, keepdims=False)
    gate_full, up_full, down_full = (
        lax.all_gather(gate_weight, "blk", axis=0, tiled=True),
        lax.all_gather(up_weight, "blk", axis=0, tiled=True),
        lax.all_gather(down_weight, "blk", axis=1, tiled=True),
    )
    states = dec_states.astype(jnp.float32)
    normed = rms_scale(states, attn_gain).astype(jnp.bfloat16)
    queries = jnp.dot(normed, query_weight, preferred_element_type=jnp.float32).astype(jnp.bfloat16)
    rows_here = queries.shape[0]
    probs = jnp.exp(capped_scores(queries, lax.all_gather(keys_local, "blk", axis=0, tiled=True)))
    numer = jnp.dot(
        probs.astype(jnp.bfloat16),
        lax.all_gather(values_local, "blk", axis=0, tiled=True),
        preferred_element_type=jnp.float32,
    )
    numer, denom = (numer, jnp.sum(probs, axis=1))
    context = (numer / denom[:, None]).astype(jnp.bfloat16)
    head_term = jnp.dot(context, out_weight, preferred_element_type=jnp.float32)
    attended = lax.psum(head_term.astype(jnp.bfloat16), "heads").astype(jnp.float32)
    residual = (states + rms_scale(attended, post_attn_gain)).astype(jnp.bfloat16)
    ffn_input = rms_scale(residual.astype(jnp.float32), ffn_gain).astype(jnp.bfloat16)
    section_size = lax.axis_size("section")
    section_index = lax.axis_index("section")
    out_rows = rows_here // lax.axis_size("heads")
    block_index = head_index * section_size + section_index
    ffn_rows = lax.all_gather(ffn_input, "section", axis=0, tiled=True)
    partner_block = head_index * section_size + (1 - section_index)
    send_start = jnp.clip(
        partner_block * out_rows - section_index * rows_here, 0, rows_here - out_rows
    )
    outgoing = lax.dynamic_slice_in_dim(residual, send_start, out_rows, 0)
    incoming = from_partner(outgoing, "section", 0)
    own_start = jnp.clip(
        block_index * out_rows - section_index * rows_here, 0, rows_here - out_rows
    )
    local_rows = lax.dynamic_slice_in_dim(residual, own_start, out_rows, 0)
    holder = block_index * out_rows // rows_here
    residual_out = jnp.where(holder == section_index, local_rows, incoming)
    gate = jnp.dot(ffn_rows, gate_full, preferred_element_type=jnp.float32)
    up_part = jnp.dot(ffn_rows, up_full, preferred_element_type=jnp.float32)
    hidden = (jax.nn.gelu(gate, approximate=True) * up_part).astype(jnp.bfloat16)
    terms = jnp.dot(hidden, down_full, preferred_element_type=jnp.float32)
    ffn_out = lax.psum_scatter(
        terms.astype(jnp.bfloat16), ("heads", "section"), scatter_dimension=0, tiled=True
    ).astype(jnp.float32)
    return (residual_out.astype(jnp.float32) + rms_scale(ffn_out, post_ffn_gain)).astype(
        jnp.bfloat16
    )


def shifted(block, axis, step):
    count = lax.axis_size(axis)
    return lax.ppermute(block, axis, [(i, (i + step) % count) for i in range(count)])


def exchanged_body(
    dec_states,
    cross_keys,
    cross_values,
    attn_gain,
    query_weight,
    out_weight,
    post_attn_gain,
    ffn_gain,
    gate_weight,
    up_weight,
    down_weight,
    post_ffn_gain,
):
    groups, blks, heads, sections = (
        lax.axis_size(axis) for axis in ("groups", "blk", "heads", "section")
    )
    g, z, h, c = (lax.axis_index(axis) for axis in ("groups", "blk", "heads", "section"))
    f32, bf16 = jnp.float32, jnp.bfloat16

    kv_index = h // GROUP
    keys_local = lax.dynamic_index_in_dim(cross_keys, kv_index, 1, keepdims=False)
    values_local = lax.dynamic_index_in_dim(cross_values, kv_index, 1, keepdims=False)
    mine = jnp.where(c == 0, keys_local, values_local)
    mine = jnp.concatenate([mine] + [shifted(mine, "blk", d) for d in range(1, blks)], axis=0)
    other = shifted(mine, "section", 1)
    keys = jnp.where(c == 0, mine, other)
    values = jnp.where(c == 0, other, mine)

    rows_here, width = dec_states.shape
    out_rows = rows_here // heads

    def owners(turn):
        route = []
        for head in range(heads):
            for core in range(sections):
                route.append((head * sections + core, core * heads + (head + turn) % heads))
        return route

    def rows_of(array, turn):
        return lax.dynamic_slice_in_dim(array, (h + turn) % heads * out_rows, out_rows, 0)

    states_own = lax.ppermute(rows_of(dec_states, 0), ("heads", "section"), owners(0))

    depth, units = gate_weight.shape
    down_t = down_weight.T
    common = units // LANE // blks * LANE
    share = depth // groups
    weights = (gate_weight, up_weight, down_t)

    def cut(names, row, rows, column, columns):
        return jnp.stack(
            [lax.dynamic_slice(weights[n], (row, column), (rows, columns)) for n in names]
        )

    def extra_column(target):
        return blks * common + target // sections * LANE

    def tile_route(step):
        route = []
        for low in range(blks):
            target = (low + step) % blks
            core = target % sections
            route.append((low * sections + core, target * sections + core))
        return route

    hand_over = []
    for low in range(blks):
        for core in range(sections):
            if core == low % sections:
                hand_over.append((low * sections + core, low * sections + 1 - core))

    full = {
        "in": jnp.zeros((2, blks * depth, sections * common + LANE), bf16),
        "out": jnp.zeros((1, blks * depth, sections * common + LANE), bf16),
    }

    def put(name, piece, row, column):
        full[name] = lax.dynamic_update_slice(full[name], piece, (0, row, column))

    kinds = {"in": (0, 1), "out": (2,)}
    has_tile = z % sections == c

    def spread(name, piece, row):
        put(name, piece, row, 0)
        put(name, shifted(piece, "section", 1), row, common)

    def spread_tile(name, piece, row):
        passed = lax.ppermute(piece, ("blk", "section"), hand_over)
        put(name, jnp.where(has_tile, piece, passed), row, sections * common)

    for name in ("in", "out"):
        names = kinds[name]
        spread(name, cut(names, 0, depth, z * common, common), z * depth)
        spread_tile(name, cut(names, 0, depth, extra_column(z), LANE), z * depth)
        for step in range(1, blks):
            target = (z + step) % blks
            source = (z - step) % blks
            piece = shifted(cut(names, g * share, share, target * common, common), "blk", step)
            tile = lax.ppermute(
                cut(names, g * share, share, extra_column(target), LANE),
                ("blk", "section"),
                tile_route(step),
            )
            spread(name, piece, source * depth + g * share)
            spread_tile(name, tile, source * depth + g * share)
            for turn in range(1, groups):
                row = source * depth + (g - turn) % groups * share
                spread(name, shifted(piece, "groups", turn), row)
                spread_tile(name, shifted(tile, "groups", turn), row)

    states = dec_states.astype(f32)
    normed = rms_scale(states, attn_gain).astype(bf16)
    queries = jnp.dot(normed, query_weight, preferred_element_type=f32).astype(bf16)
    probs = jnp.exp(capped_scores(queries, keys))
    numer = jnp.dot(probs.astype(bf16), values, preferred_element_type=f32)
    context = (numer / jnp.sum(probs, axis=1)[:, None]).astype(bf16)
    head_term = jnp.dot(context, out_weight, preferred_element_type=f32).astype(bf16)
    attended = sum(
        lax.ppermute(rows_of(head_term, turn), ("heads", "section"), owners(turn)).astype(f32)
        for turn in range(heads)
    )
    residual = (states_own.astype(f32) + rms_scale(attended, post_attn_gain)).astype(bf16)
    ffn_input = rms_scale(residual.astype(f32), ffn_gain).astype(bf16)

    slots = [ffn_input] + [shifted(ffn_input, "blk", -d) for d in range(1, blks)]
    chunks = [[slot] + [shifted(slot, "heads", -e) for e in range(1, heads)] for slot in slots]

    gate_all, up_all = full["in"][0], full["in"][1]
    down_all = full["out"][0]

    def ffn(rows):
        gate = jnp.dot(rows, gate_all, preferred_element_type=f32)
        up_part = jnp.dot(rows, up_all, preferred_element_type=f32)
        hidden = (jax.nn.gelu(gate, approximate=True) * up_part).astype(bf16)
        return lax.dot_general(
            hidden, down_all, (((1,), (1,)), ((), ())), preferred_element_type=f32
        )

    ffn_out = 0.0
    for d in (2, 1, 3, 0):
        terms = ffn(jnp.concatenate(chunks[d], axis=0)).astype(bf16)
        total = terms[:out_rows].astype(f32)
        for e in range(1, heads):
            total += shifted(terms[e * out_rows : (e + 1) * out_rows], "heads", e).astype(f32)
        if d > 0:
            total = shifted(total.astype(bf16), "blk", d).astype(f32)
        ffn_out += total
    return (residual.astype(f32) + rms_scale(ffn_out, post_ffn_gain)).astype(bf16)


def solution(mesh):
    in_specs = (
        P(("groups", "blk", "section"), None),
        P(("groups", "blk"), None, None),
        P(("groups", "blk"), None, None),
        P(),
        P(None, "heads"),
        P("heads", None),
        P(),
        P(),
        P("blk", ("heads", "section")),
        P("blk", ("heads", "section")),
        P(("heads", "section"), "blk"),
        P(),
    )
    out_specs = P(("groups", "blk", "heads", "section"), None)

    def program(*args):
        sizes = dict(mesh.shape)
        gate_weight = args[8]
        units = gate_weight.shape[1] // (sizes["heads"] * sizes["section"])
        depth = gate_weight.shape[0] // sizes["blk"]
        spare = units // LANE % sizes["blk"]
        fits = (
            sizes["section"] == 2
            and sizes["blk"] == 4
            and units % LANE == 0
            and spare * sizes["section"] == sizes["blk"]
            and depth % (16 * sizes["groups"]) == 0
        )
        body = exchanged_body if fits else gathered_body
        return jax.shard_map(
            body, mesh=mesh, in_specs=in_specs, out_specs=out_specs, check_vma=False
        )(*args)

    return program
```

```python
import jax
import jax.numpy as jnp
from jax import lax
from jax.experimental import pallas as pl
from jax.experimental.pallas import tpu as pltpu
from jax.sharding import PartitionSpec as P


HD = 256
GROUP = 2
LANE = 128


softcap_limit = 50.0


def from_partner(block, axis, bit):
    count = lax.axis_size(axis)
    route = []
    for low in range(count):
        high = low | 1 << bit
        if high != low and high < count:
            route += [(low, high), (high, low)]
    return lax.ppermute(block, axis, route)


def rms_scale(values, gain):
    return values * lax.rsqrt(jnp.mean(values * values, axis=-1, keepdims=True) + 1e-06) * gain


def capped_scores(queries, keys):
    raw = lax.dot_general(
        queries, keys, (((1,), (1,)), ((), ())), preferred_element_type=jnp.float32
    ) * HD ** (-0.5)
    return softcap_limit * jnp.tanh(raw / softcap_limit)


def gathered_body(
    dec_states,
    cross_keys,
    cross_values,
    attn_gain,
    query_weight,
    out_weight,
    post_attn_gain,
    ffn_gain,
    gate_weight,
    up_weight,
    down_weight,
    post_ffn_gain,
):
    head_index = lax.axis_index("heads")
    kv_index = head_index // GROUP
    keys_local = lax.dynamic_index_in_dim(cross_keys, kv_index, 1, keepdims=False)
    values_local = lax.dynamic_index_in_dim(cross_values, kv_index, 1, keepdims=False)
    gate_full, up_full, down_full = (
        lax.all_gather(gate_weight, "blk", axis=0, tiled=True),
        lax.all_gather(up_weight, "blk", axis=0, tiled=True),
        lax.all_gather(down_weight, "blk", axis=1, tiled=True),
    )
    states = dec_states.astype(jnp.float32)
    normed = rms_scale(states, attn_gain).astype(jnp.bfloat16)
    queries = jnp.dot(normed, query_weight, preferred_element_type=jnp.float32).astype(jnp.bfloat16)
    rows_here = queries.shape[0]
    probs = jnp.exp(capped_scores(queries, lax.all_gather(keys_local, "blk", axis=0, tiled=True)))
    numer = jnp.dot(
        probs.astype(jnp.bfloat16),
        lax.all_gather(values_local, "blk", axis=0, tiled=True),
        preferred_element_type=jnp.float32,
    )
    numer, denom = (numer, jnp.sum(probs, axis=1))
    context = (numer / denom[:, None]).astype(jnp.bfloat16)
    head_term = jnp.dot(context, out_weight, preferred_element_type=jnp.float32)
    attended = lax.psum(head_term.astype(jnp.bfloat16), "heads").astype(jnp.float32)
    residual = (states + rms_scale(attended, post_attn_gain)).astype(jnp.bfloat16)
    ffn_input = rms_scale(residual.astype(jnp.float32), ffn_gain).astype(jnp.bfloat16)
    section_size = lax.axis_size("section")
    section_index = lax.axis_index("section")
    out_rows = rows_here // lax.axis_size("heads")
    block_index = head_index * section_size + section_index
    ffn_rows = lax.all_gather(ffn_input, "section", axis=0, tiled=True)
    partner_block = head_index * section_size + (1 - section_index)
    send_start = jnp.clip(
        partner_block * out_rows - section_index * rows_here, 0, rows_here - out_rows
    )
    outgoing = lax.dynamic_slice_in_dim(residual, send_start, out_rows, 0)
    incoming = from_partner(outgoing, "section", 0)
    own_start = jnp.clip(
        block_index * out_rows - section_index * rows_here, 0, rows_here - out_rows
    )
    local_rows = lax.dynamic_slice_in_dim(residual, own_start, out_rows, 0)
    holder = block_index * out_rows // rows_here
    residual_out = jnp.where(holder == section_index, local_rows, incoming)
    gate = jnp.dot(ffn_rows, gate_full, preferred_element_type=jnp.float32)
    up_part = jnp.dot(ffn_rows, up_full, preferred_element_type=jnp.float32)
    hidden = (jax.nn.gelu(gate, approximate=True) * up_part).astype(jnp.bfloat16)
    terms = jnp.dot(hidden, down_full, preferred_element_type=jnp.float32)
    ffn_out = lax.psum_scatter(
        terms.astype(jnp.bfloat16), ("heads", "section"), scatter_dimension=0, tiled=True
    ).astype(jnp.float32)
    return (residual_out.astype(jnp.float32) + rms_scale(ffn_out, post_ffn_gain)).astype(
        jnp.bfloat16
    )


def shifted(block, axis, step):
    count = lax.axis_size(axis)
    return lax.ppermute(block, axis, [(i, (i + step) % count) for i in range(count)])


def ffn_kernel(rows_ref, weights_ref, out_ref, hidden_ref):
    rows = rows_ref[...]
    _, width, units = weights_ref.shape
    for at in range(0, units, TILE):
        to = min(at + TILE, units)
        gate = jnp.dot(rows, weights_ref[0, :, at:to], preferred_element_type=jnp.float32)
        up_part = jnp.dot(rows, weights_ref[1, :, at:to], preferred_element_type=jnp.float32)
        hidden_ref[:, at:to] = (jax.nn.gelu(gate, approximate=True) * up_part).astype(jnp.bfloat16)
    hidden = hidden_ref[...]
    for at in range(0, width, TILE):
        to = min(at + TILE, width)
        out_ref[:, at:to] = lax.dot_general(
            hidden,
            weights_ref[2, at:to, :],
            (((1,), (1,)), ((), ())),
            preferred_element_type=jnp.float32,
        ).astype(jnp.bfloat16)


def ffn(rows, weights):
    _, width, units = weights.shape
    count = rows.shape[0]
    in_vmem = pl.BlockSpec(memory_space=pltpu.VMEM)
    return pl.pallas_call(
        ffn_kernel,
        out_shape=jax.ShapeDtypeStruct((count, width), jnp.bfloat16),
        in_specs=[in_vmem, in_vmem],
        out_specs=in_vmem,
        scratch_shapes=[pltpu.VMEM((count, units), jnp.bfloat16)],
        cost_estimate=pl.CostEstimate(
            flops=6 * count * width * units,
            bytes_accessed=4 * count * width,
            transcendentals=count * units,
        ),
        compiler_params=pltpu.CompilerParams(vmem_limit_bytes=40 << 20),
        name="ffn",
    )(rows, weights)


TILE = 256
TURNS = (2, 1, 3)


def exchanged_body(
    dec_states,
    cross_keys,
    cross_values,
    attn_gain,
    query_weight,
    out_weight,
    post_attn_gain,
    ffn_gain,
    gate_weight,
    up_weight,
    down_weight,
    post_ffn_gain,
):
    blks = lax.axis_size("blk")
    g, z, h, c = (lax.axis_index(axis) for axis in ("groups", "blk", "heads", "section"))
    f32, bf16 = jnp.float32, jnp.bfloat16

    kv_index = h // GROUP
    keys_local = lax.dynamic_index_in_dim(cross_keys, kv_index, 1, keepdims=False)
    values_local = lax.dynamic_index_in_dim(cross_values, kv_index, 1, keepdims=False)
    mine = jnp.where(c == 0, keys_local, values_local)
    mine = jnp.concatenate([mine] + [shifted(mine, "blk", d) for d in range(1, blks)], axis=0)
    other = shifted(mine, "section", 1)
    keys = jnp.where(c == 0, mine, other)
    values = jnp.where(c == 0, other, mine)

    depth, units = gate_weight.shape
    piece = 2 * units // blks
    share = depth // 4
    weights = (gate_weight, up_weight, down_weight.T)

    def cut(row, rows, column, columns):
        return jnp.stack(
            [lax.dynamic_slice(w, (row, column), (rows, columns)) for w in weights]
        )

    own_quarter = cut((2 * g + c) * share, share, 0, units)
    next_quarter = shifted(cut((2 * g + 1 - c) * share, share, 0, units), "section", 1)
    low = jnp.where(c == 0, own_quarter, next_quarter)
    high = jnp.where(c == 0, next_quarter, own_quarter)

    def quarter_for(target):
        column = target % (blks // 2) * piece
        cuts = [lax.dynamic_slice_in_dim(part, column, piece, 2) for part in (low, high)]
        return jnp.where(target < blks // 2, *cuts)

    full = jnp.zeros((3, blks * depth, piece), bf16)

    def put(part, row):
        nonlocal full
        full = lax.dynamic_update_slice(full, part, (0, row, 0))

    here = cut(0, depth, z % (blks // 2) * piece, piece)
    hand_over = [(2 * b + b // (blks // 2), 2 * b + 1 - b // (blks // 2)) for b in range(blks)]
    passed = lax.ppermute(here, ("blk", "section"), hand_over)
    put(jnp.where(z // (blks // 2) == c, here, passed), z * depth)
    for step in TURNS:
        row = (z - step) % blks * depth
        part = shifted(quarter_for((z + step) % blks), "blk", step)
        across = shifted(part, "groups", 1)
        put(part, row + (2 * g + c) * share)
        put(shifted(part, "section", 1), row + (2 * g + 1 - c) * share)
        put(across, row + (2 * (1 - g) + c) * share)
        put(shifted(across, "section", 1), row + (2 * (1 - g) + 1 - c) * share)

    states = dec_states.astype(f32)
    normed = rms_scale(states, attn_gain).astype(bf16)
    queries = jnp.dot(normed, query_weight, preferred_element_type=f32).astype(bf16)
    probs = jnp.exp(capped_scores(queries, keys))
    numer = jnp.dot(probs.astype(bf16), values, preferred_element_type=f32)
    context = (numer / jnp.sum(probs, axis=1)[:, None]).astype(bf16)
    head_term = jnp.dot(context, out_weight, preferred_element_type=f32).astype(bf16)
    attended = head_term.astype(f32) + shifted(head_term, "heads", 1).astype(f32)
    residual = (states + rms_scale(attended, post_attn_gain)).astype(bf16)
    ffn_input = rms_scale(residual.astype(f32), ffn_gain).astype(bf16)

    rows_here = dec_states.shape[0]
    half = rows_here // 2
    own_half = lax.dynamic_slice_in_dim(ffn_input, h * half, half, 0)
    chunks = {0: ffn_input}
    for d in TURNS:
        mine = shifted(own_half, "blk", -d)
        other = shifted(mine, "heads", 1)
        chunks[d] = jnp.concatenate([jnp.where(h == 0, mine, other), jnp.where(h == 0, other, mine)])

    to_keeper = [(2 * (1 - core) + core, 2 * core + core) for core in range(2)]
    ffn_out = 0.0
    for d in (0, *TURNS):
        terms = ffn(chunks[d], full)
        total = terms.astype(f32)
        total += lax.ppermute(terms, ("heads", "section"), to_keeper).astype(f32)
        if d > 0:
            route = [
                ((b * 2 + core) * 2 + core, ((b + d) % blks * 2 + core) * 2 + core)
                for b in range(blks)
                for core in range(2)
            ]
            total = lax.ppermute(total.astype(bf16), ("blk", "heads", "section"), route)
            total = total.astype(f32)
        ffn_out += total
    scored = (residual.astype(f32) + rms_scale(ffn_out, post_ffn_gain)).astype(bf16)
    halves = lax.dynamic_slice_in_dim(scored, c * half, half, 0)
    handed = lax.ppermute(
        lax.dynamic_slice_in_dim(scored, (1 - c) * half, half, 0),
        ("heads", "section"),
        [(2 * core + core, 2 * core + 1 - core) for core in range(2)],
    )
    return jnp.where(h == c, halves, handed)


def solution(mesh):
    in_specs = (
        P(("groups", "blk", "section"), None),
        P(("groups", "blk"), None, None),
        P(("groups", "blk"), None, None),
        P(),
        P(None, "heads"),
        P("heads", None),
        P(),
        P(),
        P("blk", ("heads", "section")),
        P("blk", ("heads", "section")),
        P(("heads", "section"), "blk"),
        P(),
    )
    out_specs = P(("groups", "blk", "heads", "section"), None)

    def program(*args):
        sizes = dict(mesh.shape)
        gate_weight = args[8]
        units = gate_weight.shape[1] // (sizes["heads"] * sizes["section"])
        depth = gate_weight.shape[0] // sizes["blk"]
        fits = (
            sizes["groups"] == sizes["heads"] == sizes["section"] == 2
            and sizes["blk"] == 1 + len(TURNS)
            and depth % (4 * 16) == 0
            and 2 * units % (LANE * sizes["blk"]) == 0
        )
        if not fits:
            return jax.shard_map(
                gathered_body, mesh=mesh, in_specs=in_specs, out_specs=out_specs, check_vma=False
            )(*args)

        step = jax.shard_map(
            exchanged_body, mesh=mesh, in_specs=in_specs, out_specs=out_specs, check_vma=False
        )
        return step(*args)

    return program
```
